32 devices in a mesh: tiles: 8 (over z, y), freq: 4 (over x, core).
Axes of the slice: x: 2, y: 2, z: 4, core: 2. Of those that a mesh axis runs over, the one named last changes fastest.
Arguments:
- model_in: bfloat16 [4, 1024, 128], P('freq', 'tiles'), may hold values from -6 to 6
- observed: bfloat16 [4, 1024, 128], P('freq', 'tiles'), may hold values from -6 to 6
- right_factors: bfloat16 [4, 8, 2, 256, 128], P('freq', 'tiles'), may hold values from -0.375 to 0.375
- left_factors: bfloat16 [4, 8, 2, 256, 128], P('freq', 'tiles'), may hold values from -0.25 to 0.25
- tile_map: int32 [8, 2], P('tiles'), may hold values from 0 to 3, as said below
- tile_ranks: int32 [4, 8, 2], P('freq', 'tiles'), may hold values from 1 to 64
- window_mix: float32 [4, 4], replicated, may hold values from 0.1 to 0.6
Outputs:
- residual: float32 [4, 1024, 128], P('freq', 'tiles')
- gradient: float32 [4, 1024, 128], P('freq', 'tiles')
The draws below stay inside these ranges and needn't reach their ends.
Inputs may be any that keep to these rules, and one draw needn't show every extreme that they name: `tile_map`: devices 2j and 2j+1 of tiles together list every tile row 0 to 3 exactly once, 2 distinct rows each. `tile_ranks`: the rank of the tile named by tile_map in the same slot.
All inputs are finite; a program needn't handle non-finite values.
Results may differ from the reference program's by a relative error of at most 0.0042.
Values may be sent and summed in bfloat16 or wider, within the bound.
A program may use at most 64 MiB of HBM per device.

```python
import jax
import jax.numpy as jnp
from jax import lax

TS = 256
RANK = 64
SOURCES = 64
FREQS = 4
NT = 4
TPD = 2
N = 1024
N_TILES = 8


def draw_tile_map(key, part):
    keys = jax.random.split(key, NT)
    orders = jax.vmap(lambda one_key: jax.random.permutation(one_key, NT))(keys)
    return orders.reshape(N_TILES, TPD).astype(jnp.int32)


def touch_ends(result, rng, least, high):
    longest = result.shape.index(max(result.shape))
    spots = []
    for shift in (0, 1):
        where = [jax.random.randint(jax.random.fold_in(rng, axis), (), 0, length) for axis, length in enumerate(result.shape)]
        where[longest] = (where[longest] + shift) % result.shape[longest]
        spots.append(tuple(where))
    return result.at[spots[0]].set(least).at[spots[1]].set(high)


def block_levels(rng, dims, pieces, low, high):
    gain, own = 1.0, jax.random.fold_in(rng, 6)
    for axis_at, blocks in pieces:
        draws = jnp.exp(jax.random.uniform(jax.random.fold_in(own, axis_at), (blocks,), jnp.float32, low / len(pieces), high / len(pieces)))
        gain = gain * jnp.repeat(draws, dims[axis_at] // blocks).reshape([-1 if axis == axis_at else 1 for axis in range(len(dims))])
    return gain


def normal_values(stream_key, extent, scale, reach, cuts=(), kind=jnp.bfloat16):
    values = scale * jax.random.normal(stream_key, extent, jnp.float32)
    if cuts:
        values = values * block_levels(stream_key, extent, cuts, -0.22, 0.18)
    return jnp.clip(values, -reach, reach).astype(kind)


def setup_inputs(seed: int = 0) -> dict:
    seeds = jax.random.split(jax.random.key(seed), 8)
    return {
        "model_in": normal_values(seeds[0], (FREQS, N, 2 * SOURCES), 1.0, 6.0, ((0, 4), (1, 8))),
        "observed": normal_values(seeds[1], (FREQS, N, 2 * SOURCES), 1.0, 6.0, ((0, 4), (1, 8))),
        "right_factors": normal_values(seeds[2], (FREQS, N_TILES, TPD, TS, 2 * RANK), TS ** -0.5, 0.375, ((0, 4), (1, 8))),
        "left_factors": normal_values(seeds[3], (FREQS, N_TILES, TPD, TS, 2 * RANK), (2 * NT * RANK) ** -0.5, 0.25, ((0, 4), (1, 8))),
        "tile_map": draw_tile_map(jax.random.fold_in(seeds[7], 71), 0),
        "tile_ranks": touch_ends(jax.random.randint(seeds[5], (FREQS, N_TILES, TPD), 1, RANK + 1), jax.random.fold_in(seeds[5], 1), 1, RANK).astype(jnp.int32),
        "window_mix": jnp.clip(jax.random.uniform(seeds[6], (FREQS, FREQS), jnp.float32, 0.1, 0.6), 0.1, 0.6),
    }


def conjugate_apply(factor, values):
    product = jnp.einsum("tar,as->trs", factor.astype(jnp.float32), values.astype(jnp.float32))
    rank_width = factor.shape[2] // 2
    half_cols = values.shape[1] // 2
    real_part = product[:, :rank_width, :half_cols] + product[:, rank_width:, half_cols:]
    imag_part = product[:, :rank_width, half_cols:] - product[:, rank_width:, :half_cols]
    return jnp.concatenate([real_part, imag_part], axis=2)


def factor_apply(factor, coeffs):
    half_cols = coeffs.shape[2] // 2
    real_part = coeffs[:, :, :half_cols]
    imag_part = coeffs[:, :, half_cols:]
    upper_rows = jnp.concatenate([real_part, imag_part], axis=2)
    lower_rows = jnp.concatenate([-imag_part, real_part], axis=2)
    stacked = jnp.concatenate([upper_rows, lower_rows], axis=1)
    return jnp.einsum("tar,trs->as", factor.astype(jnp.float32), stacked.astype(jnp.float32))


def reference(model_in, observed, right_factors, left_factors, tile_map, tile_ranks, window_mix):
    columns = jnp.arange(N_TILES, dtype=jnp.int32) // 2
    levels = jnp.arange(RANK, dtype=jnp.int32)
    predicted = []
    rank_masks = []
    for freq_pos in range(FREQS):
        blocks = model_in[freq_pos].reshape(NT, TS, 2 * SOURCES)
        masks_now = levels[None, None, :, None] < tile_ranks[freq_pos][:, :, None, None]
        rank_masks.append(masks_now)

        def forward_one(operands):
            factor, column, keep_rows = operands
            field_block = lax.dynamic_index_in_dim(blocks, column, 0, keepdims=False)
            return jnp.where(keep_rows, conjugate_apply(factor, field_block), 0.0).astype(jnp.bfloat16)

        coeffs = lax.map(forward_one, (right_factors[freq_pos], columns, masks_now))
        coeff_grid = jnp.zeros((NT, NT, RANK, 2 * SOURCES), jnp.bfloat16).at[tile_map, columns[:, None]].set(coeffs)
        row_grid = coeff_grid.reshape(N_TILES, TPD, RANK, 2 * SOURCES)
        partials = lax.map(lambda operands: factor_apply(operands[0], operands[1]), (left_factors[freq_pos], row_grid))
        paired = partials.reshape(NT, 2, TS, 2 * SOURCES)
        predicted.append((paired[:, 0] + paired[:, 1]).reshape(N, 2 * SOURCES))
    predicted = jnp.stack(predicted)
    residual = jnp.einsum("fg,gns->fns", window_mix, predicted, precision=lax.Precision.HIGHEST) - observed.astype(jnp.float32)
    adjoint_res = jnp.einsum("gf,gns->fns", window_mix, residual, precision=lax.Precision.HIGHEST).astype(jnp.bfloat16)
    gradients = []
    for freq_pos in range(FREQS):
        blocks = adjoint_res[freq_pos].reshape(NT, TS, 2 * SOURCES)

        def adjoint_one(operands):
            factor, row_id = operands
            field_block = lax.dynamic_index_in_dim(blocks, row_id, 0, keepdims=False)
            return conjugate_apply(factor, field_block).astype(jnp.bfloat16)

        back_coeffs = lax.map(adjoint_one, (left_factors[freq_pos], columns))
        coeff_grid = back_coeffs.reshape(NT, NT, RANK, 2 * SOURCES)
        picked = jnp.where(rank_masks[freq_pos], coeff_grid[tile_map, columns[:, None]], 0.0).astype(jnp.bfloat16)
        partials = lax.map(lambda operands: factor_apply(operands[0], operands[1]), (right_factors[freq_pos], picked))
        paired = partials.reshape(NT, 2, TS, 2 * SOURCES)
        gradients.append((paired[:, 0] + paired[:, 1]).reshape(N, 2 * SOURCES))
    return residual, jnp.stack(gradients)
```

```python
import functools

import jax
import jax.numpy as jnp
from jax import lax
from jax.experimental import pallas as pl
from jax.experimental.pallas import tpu as pltpu
from jax.sharding import PartitionSpec as P

MESH = pl.DeviceIdType.MESH
F32 = jnp.float32
BF16 = jnp.bfloat16


def each(count, step):
    if count <= 8:
        for k in range(count):
            step(k)
    else:
        lax.fori_loop(0, count, lambda k, carry: (step(k), carry)[1], 0)


def total(count, term, start):
    if count <= 8:
        for k in range(count):
            start = start + term(k)
        return start
    return lax.fori_loop(0, count, lambda k, carry: carry + term(k), start)


def transposed_dot(left, right):
    return lax.dot_general(left, right, (((0,), (0,)), ((), ())), preferred_element_type=F32)


def half_sign(shape):
    lanes = lax.broadcasted_iota(jnp.int32, shape, 1)
    return jnp.where(lanes < shape[1] // 2, 1.0, -1.0).astype(F32)


def conjugate_fold(product):
    rank = product.shape[0] // 2
    low = product[rank:]
    swapped = pltpu.roll(low, low.shape[1] // 2, 1)
    return product[:rank] + half_sign(low.shape) * swapped


def stack_coeffs(coeffs):
    swapped = pltpu.roll(coeffs, coeffs.shape[1] // 2, 1)
    lower = -half_sign(coeffs.shape) * swapped
    return jnp.concatenate([coeffs, lower], axis=0).astype(BF16)


def kernel(
    n_tiles,
    n_freq,
    map_ref,
    rank_ref,
    mix_ref,
    model_ref,
    obs_ref,
    right_ref,
    left_ref,
    res_ref,
    grad_ref,
    x_other,
    obs_all,
    left_other,
    right_masked,
    right_rows,
    right_got,
    coeff_own,
    coeff_send,
    coeff_got,
    stacked,
    pred_send,
    pred_got,
    z_send,
    z_got,
    pair_send,
    pair_recv,
    obs_send,
    obs_recv,
    c_send,
    c_recv,
    p_send,
    p_recv,
    zs_send,
    zs_recv,
):
    tile = lax.axis_index("tiles")
    freq = lax.axis_index("freq")
    parity = lax.rem(tile, 2)
    block = tile // 2
    partner = block * 2 + (1 - parity)
    per_dev = right_ref.shape[2]
    rows = right_ref.shape[3]
    half = rows // 2
    width = right_ref.shape[4]
    rank_width = width // 2
    cols = model_ref.shape[2]
    n_rows = n_tiles // 2

    def tile_at(k):
        return lax.rem(tile + k, n_tiles)

    def freq_at(k):
        return lax.rem(freq + k, n_freq)

    barrier = pltpu.get_barrier_semaphore()

    def greet(k):
        pl.semaphore_signal(
            barrier, inc=1, device_id=(tile_at(k + 1), freq), device_id_type=MESH
        )

    each(n_tiles - 1, greet)
    for k in range(1, n_freq):
        pl.semaphore_signal(barrier, inc=1, device_id=(tile, freq_at(k)), device_id_type=MESH)
    pl.semaphore_wait(barrier, n_tiles - 1 + n_freq - 1)

    def copy(src, dst, send, recv, device):
        return pltpu.make_async_remote_copy(
            src_ref=src,
            dst_ref=dst,
            send_sem=send,
            recv_sem=recv,
            device_id=device,
            device_id_type=MESH,
        )

    own = pl.ds(pl.multiple_of(parity * half, half), half)
    other = pl.ds(pl.multiple_of((1 - parity) * half, half), half)

    x_copy = copy(model_ref.at[0], x_other, pair_send.at[0], pair_recv.at[0], (partner, freq))
    x_copy.start()
    left_copy = copy(
        left_ref.at[0, 0, :, other, :],
        left_other,
        pair_send.at[1],
        pair_recv.at[1],
        (partner, freq),
    )
    left_copy.start()

    def obs_copy(k, source):
        return copy(
            obs_ref.at[0],
            obs_all.at[source],
            obs_send.at[k],
            obs_recv.at[source],
            (tile, freq_at(k)),
        )

    for k in range(1, n_freq):
        obs_copy(k, freq).start()

    lane = lax.rem(lax.broadcasted_iota(jnp.int32, (rows, width), 1), rank_width)

    def mask_right(s):
        keep = lane < rank_ref[0, 0, s]
        right_masked[s] = jnp.where(keep, right_ref[0, 0, s].astype(F32), 0.0).astype(BF16)

    each(per_dev, mask_right)

    x_copy.wait_recv()

    def right_coeffs(s):
        product = transposed_dot(right_masked[s, own, :], model_ref[0]) + transposed_dot(
            right_masked[s, other, :], x_other[...]
        )
        coeff_own[s] = conjugate_fold(product).astype(BF16)

    each(per_dev, right_coeffs)

    def place_coeffs(i):
        def term(s):
            hit = jnp.full((rank_width, cols), map_ref[0, s], jnp.int32) == i
            return jnp.where(hit, coeff_own[s].astype(F32), 0.0)

        coeff_send[i] = total(per_dev, term, jnp.zeros((rank_width, cols), F32)).astype(BF16)

    each(n_rows, place_coeffs)

    def c_copy(k, source):
        target = tile_at(k + 1)
        return copy(
            coeff_send.at[target // 2],
            coeff_got.at[source],
            c_send.at[k],
            c_recv.at[source],
            (target, freq),
        )

    each(n_tiles - 1, lambda k: c_copy(k, tile).start())
    coeff_got[tile] = coeff_send[block]

    def place_right(i):
        def term(rows_at):
            def one(s):
                hit = jnp.full((half, width), map_ref[0, s], jnp.int32) == i
                return jnp.where(hit, right_masked[s, rows_at, :].astype(F32), 0.0)

            return total(per_dev, one, jnp.zeros((half, width), F32)).astype(BF16)

        right_rows[0, i] = term(own)
        right_rows[1, i] = term(other)

    each(n_rows, place_right)
    right_copy = copy(
        right_rows.at[1], right_got, pair_send.at[2], pair_recv.at[2], (partner, freq)
    )

    left_copy.wait_recv()
    each(n_tiles - 1, lambda k: c_copy(k, tile_at(k + 1)).wait_recv())

    def stack_forward(j):
        both = coeff_got[2 * j].astype(F32) + coeff_got[2 * j + 1].astype(F32)
        stacked[j] = stack_coeffs(both)

    each(n_rows, stack_forward)

    def forward_term(s):
        mine = jnp.dot(
            left_ref[0, 0, s, own, :],
            stacked[parity * per_dev + s],
            preferred_element_type=F32,
        )
        theirs = jnp.dot(
            left_other[s], stacked[(1 - parity) * per_dev + s], preferred_element_type=F32
        )
        return mine + theirs

    pred = total(per_dev, forward_term, jnp.zeros((half, cols), F32))
    pred_send[...] = pred.astype(BF16)

    def p_copy(k, source):
        return copy(
            pred_send,
            pred_got.at[source],
            p_send.at[k],
            p_recv.at[source],
            (tile, freq_at(k)),
        )

    for k in range(1, n_freq):
        p_copy(k, freq).start()
    right_copy.start()

    res = mix_ref[freq, freq] * pred - obs_ref[0].astype(F32)

    def gram(at):
        weight = mix_ref[0, freq] * mix_ref[0, at]
        for g in range(1, n_freq):
            weight = weight + mix_ref[g, freq] * mix_ref[g, at]
        return weight

    adjoint = gram(freq) * pred - mix_ref[freq, freq] * obs_ref[0].astype(F32)
    for k in range(1, n_freq):
        source = freq_at(k)
        obs_copy(k, source).wait_recv()
        adjoint = adjoint - mix_ref[source, freq] * obs_all[source].astype(F32)
    for k in range(1, n_freq):
        source = freq_at(k)
        p_copy(k, source).wait_recv()
        got = pred_got[source].astype(F32)
        res = res + mix_ref[freq, source] * got
        adjoint = adjoint + gram(source) * got
    adjoint_bf = adjoint.astype(BF16)

    def back(s):
        mine = transposed_dot(left_ref[0, 0, s, own, :], adjoint_bf)
        z_send[parity * per_dev + s] = conjugate_fold(mine).astype(BF16)
        theirs = transposed_dot(left_other[s], adjoint_bf)
        z_send[(1 - parity) * per_dev + s] = conjugate_fold(theirs).astype(BF16)

    each(per_dev, back)

    def z_copy(k, source):
        target = tile_at(k + 1)
        return copy(
            z_send.at[target // 2],
            z_got.at[source],
            zs_send.at[k],
            zs_recv.at[source],
            (target, freq),
        )

    each(n_tiles - 1, lambda k: z_copy(k, tile).start())
    z_got[tile] = z_send[block]
    res_ref[0] = res

    right_copy.wait_recv()

    def merge_right(i):
        right_rows[0, i] = (right_rows[0, i].astype(F32) + right_got[i].astype(F32)).astype(BF16)

    each(n_rows, merge_right)
    each(n_tiles - 1, lambda k: z_copy(k, tile_at(k + 1)).wait_recv())

    def gradient_term(i):
        both = z_got[2 * i].astype(F32) + z_got[2 * i + 1].astype(F32)
        return jnp.dot(right_rows[0, i], stack_coeffs(both), preferred_element_type=F32)

    grad_ref[0] = total(n_rows, gradient_term, jnp.zeros((half, cols), F32))

    x_copy.wait_send()
    left_copy.wait_send()
    right_copy.wait_send()
    for k in range(1, n_freq):
        obs_copy(k, freq).wait_send()
        p_copy(k, freq).wait_send()
    each(n_tiles - 1, lambda k: c_copy(k, tile).wait_send())
    each(n_tiles - 1, lambda k: z_copy(k, tile).wait_send())


def body(model_in, observed, right_factors, left_factors, tile_map, tile_ranks, window_mix):
    n_tiles = lax.axis_size("tiles")
    n_freq = lax.axis_size("freq")
    n_rows = n_tiles // 2
    per_dev, rows, width = right_factors.shape[2:]
    half = rows // 2
    cols = model_in.shape[2]
    rank = width // 2
    vmem = pl.BlockSpec(memory_space=pltpu.VMEM)
    smem = pl.BlockSpec(memory_space=pltpu.SMEM)
    dma = pltpu.SemaphoreType.DMA
    field = jax.ShapeDtypeStruct((1, half, cols), F32)
    return pl.pallas_call(
        functools.partial(kernel, n_tiles, n_freq),
        out_shape=(field, field),
        in_specs=[smem, smem, smem, vmem, vmem, vmem, vmem],
        out_specs=(vmem, vmem),
        scratch_shapes=[
            pltpu.VMEM((half, cols), BF16),
            pltpu.VMEM((n_freq, half, cols), BF16),
            pltpu.VMEM((per_dev, half, width), BF16),
            pltpu.VMEM((per_dev, rows, width), BF16),
            pltpu.VMEM((2, n_rows, half, width), BF16),
            pltpu.VMEM((n_rows, half, width), BF16),
            pltpu.VMEM((per_dev, rank, cols), BF16),
            pltpu.VMEM((n_rows, rank, cols), BF16),
            pltpu.VMEM((n_tiles, rank, cols), BF16),
            pltpu.VMEM((n_rows, width, cols), BF16),
            pltpu.VMEM((half, cols), BF16),
            pltpu.VMEM((n_freq, half, cols), BF16),
            pltpu.VMEM((n_rows, rank, cols), BF16),
            pltpu.VMEM((n_tiles, rank, cols), BF16),
            dma((3,)),
            dma((3,)),
            dma((n_freq,)),
            dma((n_freq,)),
            dma((n_tiles,)),
            dma((n_tiles,)),
            dma((n_freq,)),
            dma((n_freq,)),
            dma((n_tiles,)),
            dma((n_tiles,)),
        ],
        compiler_params=pltpu.CompilerParams(
            collective_id=0, has_side_effects=True, vmem_limit_bytes=40 * 1024 * 1024
        ),
        name="deconvolve",
    )(tile_map, tile_ranks, window_mix, model_in, observed, right_factors, left_factors)


def solution(mesh):
    placed = (
        P("freq", "tiles", None),
        P("freq", "tiles", None),
        P("freq", "tiles", None, None, None),
        P("freq", "tiles", None, None, None),
        P("tiles", None),
        P("freq", "tiles", None),
        P(),
    )
    return jax.shard_map(
        body,
        mesh=mesh,
        in_specs=placed,
        out_specs=(P("freq", "tiles", None), P("freq", "tiles", None)),
        check_vma=False,
    )
```

```python
import functools

import jax
import jax.numpy as jnp
from jax import lax
from jax.experimental import pallas as pl
from jax.experimental.pallas import tpu as pltpu
from jax.sharding import PartitionSpec as P

MESH = pl.DeviceIdType.MESH
F32 = jnp.float32
BF16 = jnp.bfloat16


def each(count, step):
    if count <= 8:
        for k in range(count):
            step(k)
    else:
        lax.fori_loop(0, count, lambda k, carry: (step(k), carry)[1], 0)


def total(count, term, start):
    if count <= 8:
        for k in range(count):
            start = start + term(k)
        return start
    return lax.fori_loop(0, count, lambda k, carry: carry + term(k), start)


def transposed_dot(left, right):
    return lax.dot_general(left, right, (((0,), (0,)), ((), ())), preferred_element_type=F32)


def half_sign(shape):
    lanes = lax.broadcasted_iota(jnp.int32, shape, 1)
    return jnp.where(lanes < shape[1] // 2, 1.0, -1.0).astype(F32)


def conjugate_fold(product):
    rank = product.shape[0] // 2
    low = product[rank:]
    swapped = pltpu.roll(low, low.shape[1] // 2, 1)
    return product[:rank] + half_sign(low.shape) * swapped


def stack_coeffs(coeffs):
    swapped = pltpu.roll(coeffs, coeffs.shape[1] // 2, 1)
    lower = -half_sign(coeffs.shape) * swapped
    return jnp.concatenate([coeffs, lower], axis=0).astype(BF16)


def kernel(
    n_tiles,
    n_freq,
    map_hbm,
    rank_hbm,
    mix_hbm,
    model_hbm,
    obs_hbm,
    right_hbm,
    left_hbm,
    res_ref,
    grad_ref,
    map_ref,
    rank_ref,
    mix_ref,
    model_ref,
    obs_ref,
    right_ref,
    left_ref,
    in_sem,
    x_other,
    obs_all,
    left_other,
    right_masked,
    right_rows,
    right_got,
    coeff_own,
    coeff_send,
    coeff_got,
    stacked,
    pred_send,
    pred_got,
    z_send,
    z_got,
    pair_send,
    pair_recv,
    obs_send,
    obs_recv,
    c_send,
    c_recv,
    p_send,
    p_recv,
    zs_send,
    zs_recv,
):
    tile = lax.axis_index("tiles")
    freq = lax.axis_index("freq")
    parity = lax.rem(tile, 2)
    block = tile // 2
    partner = block * 2 + (1 - parity)
    per_dev = right_ref.shape[2]
    rows = right_ref.shape[3]
    half = rows // 2
    width = right_ref.shape[4]
    rank_width = width // 2
    cols = model_ref.shape[2]
    n_rows = n_tiles // 2

    def tile_at(k):
        return lax.rem(tile + k, n_tiles)

    def freq_at(k):
        return lax.rem(freq + k, n_freq)

    inputs = [
        pltpu.make_async_copy(src, dst, in_sem.at[at])
        for at, (src, dst) in enumerate(
            [
                (right_hbm, right_ref),
                (rank_hbm, rank_ref),
                (model_hbm, model_ref),
                (map_hbm, map_ref),
                (left_hbm, left_ref),
                (obs_hbm, obs_ref),
                (mix_hbm, mix_ref),
            ]
        )
    ]
    barrier = pltpu.get_barrier_semaphore()

    def greet(k):
        pl.semaphore_signal(
            barrier, inc=1, device_id=(tile_at(k + 1), freq), device_id_type=MESH
        )

    each(n_tiles - 1, greet)
    for k in range(1, n_freq):
        pl.semaphore_signal(barrier, inc=1, device_id=(tile, freq_at(k)), device_id_type=MESH)
    for one in inputs:
        one.start()
    inputs[0].wait()
    inputs[1].wait()
    lane = lax.rem(lax.broadcasted_iota(jnp.int32, (rows, width), 1), rank_width)

    def mask_right(s):
        keep = lane < rank_ref[0, 0, s]
        right_masked[s] = jnp.where(keep, right_ref[0, 0, s].astype(F32), 0.0).astype(BF16)

    each(per_dev, mask_right)
    pl.semaphore_wait(barrier, n_tiles - 1 + n_freq - 1)

    def copy(src, dst, send, recv, device):
        return pltpu.make_async_remote_copy(
            src_ref=src,
            dst_ref=dst,
            send_sem=send,
            recv_sem=recv,
            device_id=device,
            device_id_type=MESH,
        )

    own = pl.ds(pl.multiple_of(parity * half, half), half)
    other = pl.ds(pl.multiple_of((1 - parity) * half, half), half)

    x_copy = copy(model_hbm.at[0], x_other, pair_send.at[0], pair_recv.at[0], (partner, freq))
    x_copy.start()
    left_copy = copy(
        left_hbm.at[0, 0, :, other, :],
        left_other,
        pair_send.at[1],
        pair_recv.at[1],
        (partner, freq),
    )
    left_copy.start()

    def obs_copy(k, source):
        return copy(
            obs_hbm.at[0],
            obs_all.at[source],
            obs_send.at[k],
            obs_recv.at[source],
            (tile, freq_at(k)),
        )

    for k in range(1, n_freq):
        obs_copy(k, freq).start()

    inputs[2].wait()
    inputs[3].wait()
    x_copy.wait_recv()

    def right_coeffs(s):
        product = transposed_dot(right_masked[s, own, :], model_ref[0]) + transposed_dot(
            right_masked[s, other, :], x_other[...]
        )
        coeff_own[s] = conjugate_fold(product).astype(BF16)

    each(per_dev, right_coeffs)

    def place_coeffs(i):
        def term(s):
            hit = jnp.full((rank_width, cols), map_ref[0, s], jnp.int32) == i
            return jnp.where(hit, coeff_own[s].astype(F32), 0.0)

        coeff_send[i] = total(per_dev, term, jnp.zeros((rank_width, cols), F32)).astype(BF16)

    each(n_rows, place_coeffs)

    def c_copy(k, source):
        target = tile_at(k + 1)
        return copy(
            coeff_send.at[target // 2],
            coeff_got.at[source],
            c_send.at[k],
            c_recv.at[source],
            (target, freq),
        )

    each(n_tiles - 1, lambda k: c_copy(k, tile).start())
    coeff_got[tile] = coeff_send[block]

    def place_right(i):
        def term(rows_at):
            def one(s):
                hit = jnp.full((half, width), map_ref[0, s], jnp.int32) == i
                return jnp.where(hit, right_masked[s, rows_at, :].astype(F32), 0.0)

            return total(per_dev, one, jnp.zeros((half, width), F32)).astype(BF16)

        right_rows[0, i] = term(own)
        right_rows[1, i] = term(other)

    each(n_rows, place_right)
    right_copy = copy(
        right_rows.at[1], right_got, pair_send.at[2], pair_recv.at[2], (partner, freq)
    )

    for one in inputs[4:]:
        one.wait()
    left_copy.wait_recv()
    each(n_tiles - 1, lambda k: c_copy(k, tile_at(k + 1)).wait_recv())

    def stack_forward(j):
        both = coeff_got[2 * j].astype(F32) + coeff_got[2 * j + 1].astype(F32)
        stacked[j] = stack_coeffs(both)

    each(n_rows, stack_forward)

    def forward_term(s):
        mine = jnp.dot(
            left_ref[0, 0, s, own, :],
            stacked[parity * per_dev + s],
            preferred_element_type=F32,
        )
        theirs = jnp.dot(
            left_other[s], stacked[(1 - parity) * per_dev + s], preferred_element_type=F32
        )
        return mine + theirs

    pred = total(per_dev, forward_term, jnp.zeros((half, cols), F32))
    pred_send[...] = pred.astype(BF16)

    def p_copy(k, source):
        return copy(
            pred_send,
            pred_got.at[source],
            p_send.at[k],
            p_recv.at[source],
            (tile, freq_at(k)),
        )

    for k in range(1, n_freq):
        p_copy(k, freq).start()
    right_copy.start()

    res = mix_ref[freq, freq] * pred - obs_ref[0].astype(F32)

    def gram(at):
        weight = mix_ref[0, freq] * mix_ref[0, at]
        for g in range(1, n_freq):
            weight = weight + mix_ref[g, freq] * mix_ref[g, at]
        return weight

    adjoint = gram(freq) * pred - mix_ref[freq, freq] * obs_ref[0].astype(F32)
    for k in range(1, n_freq):
        source = freq_at(k)
        obs_copy(k, source).wait_recv()
        adjoint = adjoint - mix_ref[source, freq] * obs_all[source].astype(F32)
    for k in range(1, n_freq):
        source = freq_at(k)
        p_copy(k, source).wait_recv()
        got = pred_got[source].astype(F32)
        res = res + mix_ref[freq, source] * got
        adjoint = adjoint + gram(source) * got
    adjoint_bf = adjoint.astype(BF16)

    def back(s):
        mine = transposed_dot(left_ref[0, 0, s, own, :], adjoint_bf)
        z_send[parity * per_dev + s] = conjugate_fold(mine).astype(BF16)
        theirs = transposed_dot(left_other[s], adjoint_bf)
        z_send[(1 - parity) * per_dev + s] = conjugate_fold(theirs).astype(BF16)

    each(per_dev, back)

    def z_copy(k, source):
        target = tile_at(k + 1)
        return copy(
            z_send.at[target // 2],
            z_got.at[source],
            zs_send.at[k],
            zs_recv.at[source],
            (target, freq),
        )

    each(n_tiles - 1, lambda k: z_copy(k, tile).start())
    z_got[tile] = z_send[block]
    res_ref[0] = res

    right_copy.wait_recv()

    def merge_right(i):
        right_rows[0, i] = (right_rows[0, i].astype(F32) + right_got[i].astype(F32)).astype(BF16)

    each(n_rows, merge_right)
    each(n_tiles - 1, lambda k: z_copy(k, tile_at(k + 1)).wait_recv())

    def gradient_term(i):
        both = z_got[2 * i].astype(F32) + z_got[2 * i + 1].astype(F32)
        return jnp.dot(right_rows[0, i], stack_coeffs(both), preferred_element_type=F32)

    grad_ref[0] = total(n_rows, gradient_term, jnp.zeros((half, cols), F32))

    x_copy.wait_send()
    left_copy.wait_send()
    right_copy.wait_send()
    for k in range(1, n_freq):
        obs_copy(k, freq).wait_send()
        p_copy(k, freq).wait_send()
    each(n_tiles - 1, lambda k: c_copy(k, tile).wait_send())
    each(n_tiles - 1, lambda k: z_copy(k, tile).wait_send())


def body(model_in, observed, right_factors, left_factors, tile_map, tile_ranks, window_mix):
    n_tiles = lax.axis_size("tiles")
    n_freq = lax.axis_size("freq")
    n_rows = n_tiles // 2
    per_dev, rows, width = right_factors.shape[2:]
    half = rows // 2
    cols = model_in.shape[2]
    rank = width // 2
    vmem = pl.BlockSpec(memory_space=pltpu.VMEM)
    hbm = pl.BlockSpec(memory_space=pl.ANY)
    dma = pltpu.SemaphoreType.DMA
    field = jax.ShapeDtypeStruct((1, half, cols), F32)
    return pl.pallas_call(
        functools.partial(kernel, n_tiles, n_freq),
        out_shape=(field, field),
        in_specs=[hbm] * 7,
        out_specs=(vmem, vmem),
        scratch_shapes=[
            pltpu.SMEM(tile_map.shape, jnp.int32),
            pltpu.SMEM(tile_ranks.shape, jnp.int32),
            pltpu.SMEM(window_mix.shape, F32),
            pltpu.VMEM(model_in.shape, BF16),
            pltpu.VMEM(observed.shape, BF16),
            pltpu.VMEM(right_factors.shape, BF16),
            pltpu.VMEM(left_factors.shape, BF16),
            dma((7,)),
            pltpu.VMEM((half, cols), BF16),
            pltpu.VMEM((n_freq, half, cols), BF16),
            pltpu.VMEM((per_dev, half, width), BF16),
            pltpu.VMEM((per_dev, rows, width), BF16),
            pltpu.VMEM((2, n_rows, half, width), BF16),
            pltpu.VMEM((n_rows, half, width), BF16),
            pltpu.VMEM((per_dev, rank, cols), BF16),
            pltpu.VMEM((n_rows, rank, cols), BF16),
            pltpu.VMEM((n_tiles, rank, cols), BF16),
            pltpu.VMEM((n_rows, width, cols), BF16),
            pltpu.VMEM((half, cols), BF16),
            pltpu.VMEM((n_freq, half, cols), BF16),
            pltpu.VMEM((n_rows, rank, cols), BF16),
            pltpu.VMEM((n_tiles, rank, cols), BF16),
            dma((3,)),
            dma((3,)),
            dma((n_freq,)),
            dma((n_freq,)),
            dma((n_tiles,)),
            dma((n_tiles,)),
            dma((n_freq,)),
            dma((n_freq,)),
            dma((n_tiles,)),
            dma((n_tiles,)),
        ],
        compiler_params=pltpu.CompilerParams(
            collective_id=0, has_side_effects=True, vmem_limit_bytes=62 * 1024 * 1024
        ),
        name="deconvolve",
    )(tile_map, tile_ranks, window_mix, model_in, observed, right_factors, left_factors)


def solution(mesh):
    placed = (
        P("freq", "tiles", None),
        P("freq", "tiles", None),
        P("freq", "tiles", None, None, None),
        P("freq", "tiles", None, None, None),
        P("tiles", None),
        P("freq", "tiles", None),
        P(),
    )
    return jax.shard_map(
        body,
        mesh=mesh,
        in_specs=placed,
        out_specs=(P("freq", "tiles", None), P("freq", "tiles", None)),
        check_vma=False,
    )
```

```python
import functools

import jax
import jax.numpy as jnp
from jax import lax
from jax.experimental import pallas as pl
from jax.experimental.pallas import tpu as pltpu
from jax.sharding import PartitionSpec as P

MESH = pl.DeviceIdType.MESH
F32 = jnp.float32
BF16 = jnp.bfloat16


def each(count, step):
    if count <= 8:
        for k in range(count):
            step(k)
    else:
        lax.fori_loop(0, count, lambda k, carry: (step(k), carry)[1], 0)


def total(count, term, start):
    if count <= 8:
        for k in range(count):
            start = start + term(k)
        return start
    return lax.fori_loop(0, count, lambda k, carry: carry + term(k), start)


def transposed_dot(left, right):
    return lax.dot_general(left, right, (((0,), (0,)), ((), ())), preferred_element_type=F32)


def half_sign(shape):
    lanes = lax.broadcasted_iota(jnp.int32, shape, 1)
    return jnp.where(lanes < shape[1] // 2, 1.0, -1.0).astype(F32)


def conjugate_fold(product):
    rank = product.shape[0] // 2
    low = product[rank:]
    swapped = pltpu.roll(low, low.shape[1] // 2, 1)
    return product[:rank] + half_sign(low.shape) * swapped


def stack_coeffs(coeffs):
    swapped = pltpu.roll(coeffs, coeffs.shape[1] // 2, 1)
    lower = -half_sign(coeffs.shape) * swapped
    return jnp.concatenate([coeffs, lower], axis=0).astype(BF16)


def kernel(
    n_tiles,
    n_freq,
    map_hbm,
    rank_hbm,
    mix_hbm,
    model_hbm,
    obs_hbm,
    right_hbm,
    left_hbm,
    res_ref,
    grad_ref,
    map_ref,
    rank_ref,
    mix_ref,
    model_ref,
    obs_ref,
    right_ref,
    left_ref,
    in_sem,
    x_other,
    obs_all,
    left_other,
    right_masked,
    right_rows,
    right_got,
    coeff_own,
    coeff_send,
    coeff_got,
    stacked,
    pred_send,
    pred_got,
    z_send,
    z_got,
    pair_send,
    pair_recv,
    obs_send,
    obs_recv,
    c_send,
    c_recv,
    p_send,
    p_recv,
    zs_send,
    zs_recv,
):
    tile = lax.axis_index("tiles")
    freq = lax.axis_index("freq")
    parity = lax.rem(tile, 2)
    block = tile // 2
    partner = block * 2 + (1 - parity)
    per_dev = right_ref.shape[2]
    rows = right_ref.shape[3]
    half = rows // 2
    width = right_ref.shape[4]
    rank_width = width // 2
    cols = model_ref.shape[2]
    n_rows = n_tiles // 2

    def tile_at(k):
        return lax.rem(tile + k, n_tiles)

    def freq_at(k):
        return lax.rem(freq + k, n_freq)

    inputs = [
        pltpu.make_async_copy(src, dst, in_sem.at[at])
        for at, (src, dst) in enumerate(
            [
                (right_hbm, right_ref),
                (rank_hbm, rank_ref),
                (model_hbm, model_ref),
                (map_hbm, map_ref),
                (left_hbm, left_ref),
                (obs_hbm, obs_ref),
                (mix_hbm, mix_ref),
            ]
        )
    ]
    barrier = pltpu.get_barrier_semaphore()

    def greet(k):
        pl.semaphore_signal(
            barrier, inc=1, device_id=(tile_at(k + 1), freq), device_id_type=MESH
        )

    each(n_tiles - 1, greet)
    for k in range(1, n_freq):
        pl.semaphore_signal(barrier, inc=1, device_id=(tile, freq_at(k)), device_id_type=MESH)
    for one in inputs:
        one.start()
    inputs[0].wait()
    inputs[1].wait()
    lane = lax.rem(lax.broadcasted_iota(jnp.int32, (rows, width), 1), rank_width)

    def mask_right(s):
        keep = lane < rank_ref[0, 0, s]
        right_masked[s] = jnp.where(keep, right_ref[0, 0, s].astype(F32), 0.0).astype(BF16)

    each(per_dev, mask_right)
    pl.semaphore_wait(barrier, n_tiles - 1 + n_freq - 1)

    def copy(src, dst, send, recv, device):
        return pltpu.make_async_remote_copy(
            src_ref=src,
            dst_ref=dst,
            send_sem=send,
            recv_sem=recv,
            device_id=device,
            device_id_type=MESH,
        )

    own = pl.ds(pl.multiple_of(parity * half, half), half)
    other = pl.ds(pl.multiple_of((1 - parity) * half, half), half)

    x_copy = copy(model_hbm.at[0], x_other, pair_send.at[0], pair_recv.at[0], (partner, freq))
    x_copy.start()
    left_copy = copy(
        left_hbm.at[0, 0, :, other, :],
        left_other,
        pair_send.at[1],
        pair_recv.at[1],
        (partner, freq),
    )
    left_copy.start()

    def obs_copy(k, source):
        return copy(
            obs_hbm.at[0],
            obs_all.at[source],
            obs_send.at[k],
            obs_recv.at[source],
            (tile, freq_at(k)),
        )

    for k in range(1, n_freq):
        obs_copy(k, freq).start()

    inputs[2].wait()
    inputs[3].wait()
    x_copy.wait_recv()

    def right_coeffs(s):
        product = transposed_dot(right_masked[s, own, :], model_ref[0]) + transposed_dot(
            right_masked[s, other, :], x_other[...]
        )
        coeff_own[s] = conjugate_fold(product).astype(BF16)

    each(per_dev, right_coeffs)

    def place_coeffs(i):
        def term(s):
            hit = jnp.full((rank_width, cols), map_ref[0, s], jnp.int32) == i
            return jnp.where(hit, coeff_own[s].astype(F32), 0.0)

        coeff_send[i] = total(per_dev, term, jnp.zeros((rank_width, cols), F32)).astype(BF16)

    each(n_rows, place_coeffs)

    def c_copy(k, source):
        target = tile_at(k + 1)
        return copy(
            coeff_send.at[target // 2],
            coeff_got.at[source],
            c_send.at[k],
            c_recv.at[source],
            (target, freq),
        )

    each(n_tiles - 1, lambda k: c_copy(k, tile).start())
    coeff_got[tile] = coeff_send[block]

    def place_right(i):
        def term(rows_at):
            def one(s):
                hit = jnp.full((half, width), map_ref[0, s], jnp.int32) == i
                return jnp.where(hit, right_masked[s, rows_at, :].astype(F32), 0.0)

            return total(per_dev, one, jnp.zeros((half, width), F32)).astype(BF16)

        right_rows[0, i] = term(own)
        right_rows[1, i] = term(other)

    each(n_rows, place_right)
    right_copy = copy(
        right_rows.at[1], right_got, pair_send.at[2], pair_recv.at[2], (partner, freq)
    )

    for one in inputs[4:]:
        one.wait()
    left_copy.wait_recv()
    each(n_tiles - 1, lambda k: c_copy(k, tile_at(k + 1)).wait_recv())

    def stack_forward(j):
        both = coeff_got[2 * j].astype(F32) + coeff_got[2 * j + 1].astype(F32)
        stacked[j] = stack_coeffs(both)

    each(n_rows, stack_forward)

    def forward_term(s):
        mine = jnp.dot(
            left_ref[0, 0, s, own, :],
            stacked[parity * per_dev + s],
            preferred_element_type=F32,
        )
        theirs = jnp.dot(
            left_other[s], stacked[(1 - parity) * per_dev + s], preferred_element_type=F32
        )
        return mine + theirs

    pred = total(per_dev, forward_term, jnp.zeros((half, cols), F32))
    pred_send[...] = pred.astype(BF16)

    def p_copy(k, source):
        return copy(
            pred_send,
            pred_got.at[source],
            p_send.at[k],
            p_recv.at[source],
            (tile, freq_at(k)),
        )

    for k in range(1, n_freq):
        p_copy(k, freq).start()
    right_copy.start()

    res = mix_ref[freq, freq] * pred - obs_ref[0].astype(F32)

    def gram(at):
        weight = mix_ref[0, freq] * mix_ref[0, at]
        for g in range(1, n_freq):
            weight = weight + mix_ref[g, freq] * mix_ref[g, at]
        return weight

    adjoint = gram(freq) * pred - mix_ref[freq, freq] * obs_ref[0].astype(F32)
    for k in range(1, n_freq):
        source = freq_at(k)
        obs_copy(k, source).wait_recv()
        adjoint = adjoint - mix_ref[source, freq] * obs_all[source].astype(F32)
    for k in range(1, n_freq):
        source = freq_at(k)
        p_copy(k, source).wait_recv()
        got = pred_got[source].astype(F32)
        res = res + mix_ref[freq, source] * got
        adjoint = adjoint + gram(source) * got
    adjoint_bf = adjoint.astype(BF16)

    def back(s):
        mine = transposed_dot(left_ref[0, 0, s, own, :], adjoint_bf)
        z_send[parity * per_dev + s] = conjugate_fold(mine).astype(BF16)
        theirs = transposed_dot(left_other[s], adjoint_bf)
        z_send[(1 - parity) * per_dev + s] = conjugate_fold(theirs).astype(BF16)

    each(per_dev, back)

    def z_copy(k, source):
        target = tile_at(k + 1)
        return copy(
            z_send.at[target // 2],
            z_got.at[source],
            zs_send.at[k],
            zs_recv.at[source],
            (target, freq),
        )

    each(n_tiles - 1, lambda k: z_copy(k, tile).start())
    z_got[tile] = z_send[block]
    res_ref[0] = res

    right_copy.wait_recv()

    def merge_right(i):
        right_rows[0, i] = (right_rows[0, i].astype(F32) + right_got[i].astype(F32)).astype(BF16)

    each(n_rows, merge_right)
    each(n_tiles - 1, lambda k: z_copy(k, tile_at(k + 1)).wait_recv())

    def gradient_term(i):
        both = z_got[2 * i].astype(F32) + z_got[2 * i + 1].astype(F32)
        return jnp.dot(right_rows[0, i], stack_coeffs(both), preferred_element_type=F32)

    grad_ref[0] = total(n_rows, gradient_term, jnp.zeros((half, cols), F32))

    x_copy.wait_send()
    left_copy.wait_send()
    right_copy.wait_send()
    for k in range(1, n_freq):
        obs_copy(k, freq).wait_send()
        p_copy(k, freq).wait_send()
    each(n_tiles - 1, lambda k: c_copy(k, tile).wait_send())
    each(n_tiles - 1, lambda k: z_copy(k, tile).wait_send())


def body(model_in, observed, right_factors, left_factors, tile_map, tile_ranks, window_mix):
    n_tiles = lax.axis_size("tiles")
    n_freq = lax.axis_size("freq")
    n_rows = n_tiles // 2
    per_dev, rows, width = right_factors.shape[2:]
    half = rows // 2
    cols = model_in.shape[2]
    rank = width // 2
    vmem = pl.BlockSpec(memory_space=pltpu.VMEM)
    hbm = pl.BlockSpec(memory_space=pl.ANY)
    dma = pltpu.SemaphoreType.DMA
    field = jax.ShapeDtypeStruct((1, half, cols), F32)
    return pl.pallas_call(
        functools.partial(kernel, n_tiles, n_freq),
        out_shape=(field, field),
        in_specs=[hbm] * 7,
        out_specs=(vmem, vmem),
        scratch_shapes=[
            pltpu.SMEM(tile_map.shape, jnp.int32),
            pltpu.SMEM(tile_ranks.shape, jnp.int32),
            pltpu.SMEM(window_mix.shape, F32),
            pltpu.VMEM(model_in.shape, BF16),
            pltpu.VMEM(observed.shape, BF16),
            pltpu.VMEM(right_factors.shape, BF16),
            pltpu.VMEM(left_factors.shape, BF16),
            dma((7,)),
            pltpu.VMEM((half, cols), BF16),
            pltpu.VMEM((n_freq, half, cols), BF16),
            pltpu.VMEM((per_dev, half, width), BF16),
            pltpu.VMEM((per_dev, rows, width), BF16),
            pltpu.VMEM((2, n_rows, half, width), BF16),
            pltpu.VMEM((n_rows, half, width), BF16),
            pltpu.VMEM((per_dev, rank, cols), BF16),
            pltpu.VMEM((n_rows, rank, cols), BF16),
            pltpu.VMEM((n_tiles, rank, cols), BF16),
            pltpu.VMEM((n_rows, width, cols), BF16),
            pltpu.VMEM((half, cols), BF16),
            pltpu.VMEM((n_freq, half, cols), BF16),
            pltpu.VMEM((n_rows, rank, cols), BF16),
            pltpu.VMEM((n_tiles, rank, cols), BF16),
            dma((3,)),
            dma((3,)),
            dma((n_freq,)),
            dma((n_freq,)),
            dma((n_tiles,)),
            dma((n_tiles,)),
            dma((n_freq,)),
            dma((n_freq,)),
            dma((n_tiles,)),
            dma((n_tiles,)),
        ],
        compiler_params=pltpu.CompilerParams(
            collective_id=0, has_side_effects=True, vmem_limit_bytes=40 * 1024 * 1024
        ),
        name="deconvolve",
    )(*[pltpu.with_memory_space_constraint(a, pltpu.HBM) for a in (tile_map, tile_ranks, window_mix, model_in, observed, right_factors, left_factors)])


def solution(mesh):
    placed = (
        P("freq", "tiles", None),
        P("freq", "tiles", None),
        P("freq", "tiles", None, None, None),
        P("freq", "tiles", None, None, None),
        P("tiles", None),
        P("freq", "tiles", None),
        P(),
    )
    return jax.shard_map(
        body,
        mesh=mesh,
        in_specs=placed,
        out_specs=(P("freq", "tiles", None), P("freq", "tiles", None)),
        check_vma=False,
    )
```

```python
import functools

import jax
import jax.numpy as jnp
from jax import lax
from jax.experimental import pallas as pl
from jax.experimental.pallas import tpu as pltpu
from jax.sharding import PartitionSpec as P

MESH = pl.DeviceIdType.MESH
F32 = jnp.float32
BF16 = jnp.bfloat16


def each(count, step):
    if count <= 8:
        for k in range(count):
            step(k)
    else:
        lax.fori_loop(0, count, lambda k, carry: (step(k), carry)[1], 0)


def total(count, term, start):
    if count <= 8:
        for k in range(count):
            start = start + term(k)
        return start
    return lax.fori_loop(0, count, lambda k, carry: carry + term(k), start)


def transposed_dot(left, right):
    return lax.dot_general(left, right, (((0,), (0,)), ((), ())), preferred_element_type=F32)


def half_sign(shape):
    lanes = lax.broadcasted_iota(jnp.int32, shape, 1)
    return jnp.where(lanes < shape[1] // 2, 1.0, -1.0).astype(F32)


def conjugate_fold(product):
    rank = product.shape[0] // 2
    low = product[rank:]
    swapped = pltpu.roll(low, low.shape[1] // 2, 1)
    return product[:rank] + half_sign(low.shape) * swapped


def stack_coeffs(coeffs):
    swapped = pltpu.roll(coeffs, coeffs.shape[1] // 2, 1)
    lower = -half_sign(coeffs.shape) * swapped
    return jnp.concatenate([coeffs, lower], axis=0).astype(BF16)


def kernel(
    n_tiles,
    n_freq,
    map_hbm,
    rank_hbm,
    mix_hbm,
    model_hbm,
    obs_hbm,
    right_hbm,
    left_hbm,
    res_ref,
    grad_ref,
    map_ref,
    rank_ref,
    mix_ref,
    model_ref,
    obs_ref,
    right_ref,
    left_rows,
    in_sem,
    x_other,
    obs_all,
    right_masked,
    right_rows,
    right_got,
    coeff_own,
    coeff_send,
    coeff_got,
    pred_send,
    pred_got,
    z_send,
    z_got,
    pair_send,
    pair_recv,
    obs_send,
    obs_recv,
    c_send,
    c_recv,
    p_send,
    p_recv,
    zs_send,
    zs_recv,
):
    tile = lax.axis_index("tiles")
    freq = lax.axis_index("freq")
    parity = lax.rem(tile, 2)
    block = tile // 2
    partner = block * 2 + (1 - parity)
    per_dev = right_ref.shape[2]
    rows = right_ref.shape[3]
    half = rows // 2
    width = right_ref.shape[4]
    rank_width = width // 2
    cols = model_ref.shape[2]
    n_rows = n_tiles // 2

    def tile_at(k):
        return lax.rem(tile + k, n_tiles)

    def freq_at(k):
        return lax.rem(freq + k, n_freq)

    def row_far(k):
        upper = block // (n_rows // 2)
        first = (1 - upper) * (n_rows - 1 - k) + upper * k
        down = (block - first + n_rows) // n_rows
        up = (first - block + n_rows) // n_rows
        return first - (1 - upper) * down + upper * up

    freq_order = sorted(range(1, n_freq), key=lambda k: abs(k - n_freq // 2))

    own = pl.ds(pl.multiple_of(parity * half, half), half)
    other = pl.ds(pl.multiple_of((1 - parity) * half, half), half)
    own_slots = pl.ds(parity * per_dev, per_dev)
    inputs = [
        pltpu.make_async_copy(src, dst, in_sem.at[at])
        for at, (src, dst) in enumerate(
            [
                (right_hbm, right_ref),
                (rank_hbm, rank_ref),
                (model_hbm, model_ref),
                (map_hbm, map_ref),
                (left_hbm.at[0, 0, :, own, :], left_rows.at[own_slots]),
                (obs_hbm, obs_ref),
                (mix_hbm, mix_ref),
            ]
        )
    ]
    barrier = pltpu.get_barrier_semaphore()

    def greet(k):
        pl.semaphore_signal(
            barrier, inc=1, device_id=(tile_at(k + 1), freq), device_id_type=MESH
        )

    each(n_tiles - 1, greet)
    for k in range(1, n_freq):
        pl.semaphore_signal(barrier, inc=1, device_id=(tile, freq_at(k)), device_id_type=MESH)
    for one in inputs:
        one.start()
    inputs[0].wait()
    inputs[1].wait()
    lane = lax.rem(lax.broadcasted_iota(jnp.int32, (rows, width), 1), rank_width)

    def mask_right(s):
        keep = lane < rank_ref[0, 0, s]
        right_masked[s] = jnp.where(keep, right_ref[0, 0, s].astype(F32), 0.0).astype(BF16)

    each(per_dev, mask_right)
    pl.semaphore_wait(barrier, n_tiles - 1 + n_freq - 1)

    def copy(src, dst, send, recv, device):
        return pltpu.make_async_remote_copy(
            src_ref=src,
            dst_ref=dst,
            send_sem=send,
            recv_sem=recv,
            device_id=device,
            device_id_type=MESH,
        )

    x_copy = copy(model_hbm.at[0], x_other, pair_send.at[0], pair_recv.at[0], (partner, freq))
    x_copy.start()
    left_copy = copy(
        left_hbm.at[0, 0, :, other, :],
        left_rows.at[own_slots],
        pair_send.at[1],
        pair_recv.at[1],
        (partner, freq),
    )
    left_copy.start()

    def obs_copy(k, source):
        return copy(
            obs_hbm.at[0],
            obs_all.at[source],
            obs_send.at[k],
            obs_recv.at[source],
            (tile, freq_at(k)),
        )

    for k in range(1, n_freq):
        obs_copy(k, freq).start()

    inputs[2].wait()
    inputs[3].wait()
    x_copy.wait_recv()

    def right_coeffs(s):
        product = transposed_dot(right_masked[s, own, :], model_ref[0]) + transposed_dot(
            right_masked[s, other, :], x_other[...]
        )
        coeff_own[s] = conjugate_fold(product).astype(BF16)

    each(per_dev, right_coeffs)

    def place_coeffs(i):
        def term(s):
            hit = jnp.full((rank_width, cols), map_ref[0, s], jnp.int32) == i
            return jnp.where(hit, coeff_own[s].astype(F32), 0.0)

        coeff_send[i] = total(per_dev, term, jnp.zeros((rank_width, cols), F32)).astype(BF16)

    def c_copy(target, source):
        return copy(
            coeff_send.at[target // 2],
            coeff_got.at[source],
            c_send.at[target],
            c_recv.at[source],
            (target, freq),
        )

    def c_start(k):
        place_coeffs(row_far(k))
        c_copy(2 * row_far(k), tile).start()
        c_copy(2 * row_far(k) + 1, tile).start()

    each(n_rows - 1, c_start)
    place_coeffs(block)
    c_copy(partner, tile).start()
    coeff_got[tile] = coeff_send[block]

    def place_right(i):
        def term(rows_at):
            def one(s):
                hit = jnp.full((half, width), map_ref[0, s], jnp.int32) == i
                return jnp.where(hit, right_masked[s, rows_at, :].astype(F32), 0.0)

            return total(per_dev, one, jnp.zeros((half, width), F32)).astype(BF16)

        right_rows[0, i] = term(own)
        right_rows[1, i] = term(other)

    each(n_rows, place_right)
    right_copy = copy(
        right_rows.at[1], right_got, pair_send.at[2], pair_recv.at[2], (partner, freq)
    )

    for one in inputs[4:]:
        one.wait()
    left_copy.wait_recv()
    def forward_term(j):
        both = coeff_got[2 * j].astype(F32) + coeff_got[2 * j + 1].astype(F32)
        return jnp.dot(left_rows[j], stack_coeffs(both), preferred_element_type=F32)

    c_copy(partner, partner).wait_recv()
    pred = forward_term(block)

    def forward_near(k):
        j = row_far(n_rows - 2 - k)
        c_copy(2 * j, 2 * j).wait_recv()
        c_copy(2 * j + 1, 2 * j + 1).wait_recv()
        return forward_term(j)

    pred = total(n_rows - 1, forward_near, pred)
    pred_send[...] = pred.astype(BF16)

    def p_copy(k, source):
        return copy(
            pred_send,
            pred_got.at[source],
            p_send.at[k],
            p_recv.at[source],
            (tile, freq_at(k)),
        )

    for k in freq_order:
        p_copy(k, freq).start()
    right_copy.start()

    res = mix_ref[freq, freq] * pred - obs_ref[0].astype(F32)

    def gram(at):
        weight = mix_ref[0, freq] * mix_ref[0, at]
        for g in range(1, n_freq):
            weight = weight + mix_ref[g, freq] * mix_ref[g, at]
        return weight

    adjoint = gram(freq) * pred - mix_ref[freq, freq] * obs_ref[0].astype(F32)
    for k in range(1, n_freq):
        source = freq_at(k)
        obs_copy(k, source).wait_recv()
        adjoint = adjoint - mix_ref[source, freq] * obs_all[source].astype(F32)
    for k in range(1, n_freq):
        source = freq_at(k)
        p_copy(k, source).wait_recv()
        got = pred_got[source].astype(F32)
        res = res + mix_ref[freq, source] * got
        adjoint = adjoint + gram(source) * got
    adjoint_bf = adjoint.astype(BF16)

    def back(j):
        product = transposed_dot(left_rows[j], adjoint_bf)
        z_send[j] = conjugate_fold(product).astype(BF16)

    def z_copy(target, source):
        return copy(
            z_send.at[target // 2],
            z_got.at[source],
            zs_send.at[target],
            zs_recv.at[source],
            (target, freq),
        )

    def z_start(k):
        j = row_far(k)
        back(j)
        z_copy(2 * j, tile).start()
        z_copy(2 * j + 1, tile).start()

    each(n_rows - 1, z_start)
    back(block)
    z_copy(partner, tile).start()
    z_got[tile] = z_send[block]
    res_ref[0] = res

    right_copy.wait_recv()

    def merge_right(i):
        right_rows[0, i] = (right_rows[0, i].astype(F32) + right_got[i].astype(F32)).astype(BF16)

    each(n_rows, merge_right)
    def gradient_term(i):
        both = z_got[2 * i].astype(F32) + z_got[2 * i + 1].astype(F32)
        return jnp.dot(right_rows[0, i], stack_coeffs(both), preferred_element_type=F32)

    z_copy(partner, partner).wait_recv()
    grad = gradient_term(block)

    def gradient_near(k):
        i = row_far(n_rows - 2 - k)
        z_copy(2 * i, 2 * i).wait_recv()
        z_copy(2 * i + 1, 2 * i + 1).wait_recv()
        return gradient_term(i)

    grad_ref[0] = total(n_rows - 1, gradient_near, grad)

    x_copy.wait_send()
    left_copy.wait_send()
    right_copy.wait_send()
    for k in range(1, n_freq):
        obs_copy(k, freq).wait_send()
        p_copy(k, freq).wait_send()
    each(n_tiles - 1, lambda k: c_copy(tile_at(k + 1), tile).wait_send())
    each(n_tiles - 1, lambda k: z_copy(tile_at(k + 1), tile).wait_send())


def body(model_in, observed, right_factors, left_factors, tile_map, tile_ranks, window_mix):
    n_tiles = lax.axis_size("tiles")
    n_freq = lax.axis_size("freq")
    n_rows = n_tiles // 2
    per_dev, rows, width = right_factors.shape[2:]
    half = rows // 2
    cols = model_in.shape[2]
    rank = width // 2
    vmem = pl.BlockSpec(memory_space=pltpu.VMEM)
    hbm = pl.BlockSpec(memory_space=pl.ANY)
    dma = pltpu.SemaphoreType.DMA
    field = jax.ShapeDtypeStruct((1, half, cols), F32)
    return pl.pallas_call(
        functools.partial(kernel, n_tiles, n_freq),
        out_shape=(field, field),
        in_specs=[hbm] * 7,
        out_specs=(vmem, vmem),
        scratch_shapes=[
            pltpu.SMEM(tile_map.shape, jnp.int32),
            pltpu.SMEM(tile_ranks.shape, jnp.int32),
            pltpu.SMEM(window_mix.shape, F32),
            pltpu.VMEM(model_in.shape, BF16),
            pltpu.VMEM(observed.shape, BF16),
            pltpu.VMEM(right_factors.shape, BF16),
            pltpu.VMEM((n_rows, half, width), BF16),
            dma((7,)),
            pltpu.VMEM((half, cols), BF16),
            pltpu.VMEM((n_freq, half, cols), BF16),
            pltpu.VMEM((per_dev, rows, width), BF16),
            pltpu.VMEM((2, n_rows, half, width), BF16),
            pltpu.VMEM((n_rows, half, width), BF16),
            pltpu.VMEM((per_dev, rank, cols), BF16),
            pltpu.VMEM((n_rows, rank, cols), BF16),
            pltpu.VMEM((n_tiles, rank, cols), BF16),
            pltpu.VMEM((half, cols), BF16),
            pltpu.VMEM((n_freq, half, cols), BF16),
            pltpu.VMEM((n_rows, rank, cols), BF16),
            pltpu.VMEM((n_tiles, rank, cols), BF16),
            dma((3,)),
            dma((3,)),
            dma((n_freq,)),
            dma((n_freq,)),
            dma((n_tiles,)),
            dma((n_tiles,)),
            dma((n_freq,)),
            dma((n_freq,)),
            dma((n_tiles,)),
            dma((n_tiles,)),
        ],
        compiler_params=pltpu.CompilerParams(
            collective_id=0, has_side_effects=True, vmem_limit_bytes=40 * 1024 * 1024
        ),
        name="deconvolve",
    )(*[pltpu.with_memory_space_constraint(a, pltpu.HBM) for a in (tile_map, tile_ranks, window_mix, model_in, observed, right_factors, left_factors)])


def solution(mesh):
    placed = (
        P("freq", "tiles", None),
        P("freq", "tiles", None),
        P("freq", "tiles", None, None, None),
        P("freq", "tiles", None, None, None),
        P("tiles", None),
        P("freq", "tiles", None),
        P(),
    )
    return jax.shard_map(
        body,
        mesh=mesh,
        in_specs=placed,
        out_specs=(P("freq", "tiles", None), P("freq", "tiles", None)),
        check_vma=False,
    )
```

```python
import functools

import jax
import jax.numpy as jnp
from jax import lax
from jax.experimental import pallas as pl
from jax.experimental.pallas import tpu as pltpu
from jax.sharding import PartitionSpec as P

MESH = pl.DeviceIdType.MESH
F32 = jnp.float32
BF16 = jnp.bfloat16


def each(count, step):
    if count <= 8:
        for k in range(count):
            step(k)
    else:
        lax.fori_loop(0, count, lambda k, carry: (step(k), carry)[1], 0)


def total(count, term, start):
    if count <= 8:
        for k in range(count):
            start = start + term(k)
        return start
    return lax.fori_loop(0, count, lambda k, carry: carry + term(k), start)


def transposed_dot(left, right):
    return lax.dot_general(left, right, (((0,), (0,)), ((), ())), preferred_element_type=F32)


def half_sign(shape):
    lanes = lax.broadcasted_iota(jnp.int32, shape, 1)
    return jnp.where(lanes < shape[1] // 2, 1.0, -1.0).astype(F32)


def conjugate_fold(product):
    rank = product.shape[0] // 2
    low = product[rank:]
    swapped = pltpu.roll(low, low.shape[1] // 2, 1)
    return product[:rank] + half_sign(low.shape) * swapped


def stack_coeffs(coeffs):
    swapped = pltpu.roll(coeffs, coeffs.shape[1] // 2, 1)
    lower = -half_sign(coeffs.shape) * swapped
    return jnp.concatenate([coeffs, lower], axis=0).astype(BF16)


def kernel(
    n_tiles,
    n_freq,
    map_hbm,
    rank_hbm,
    mix_hbm,
    model_hbm,
    obs_hbm,
    right_hbm,
    left_hbm,
    res_ref,
    grad_ref,
    map_ref,
    rank_ref,
    mix_ref,
    model_ref,
    obs_ref,
    right_ref,
    left_rows,
    in_sem,
    x_other,
    obs_all,
    right_masked,
    right_rows,
    right_got,
    coeff_own,
    coeff_send,
    coeff_got,
    pred_send,
    pred_got,
    z_send,
    z_got,
    pair_send,
    pair_recv,
    obs_send,
    obs_recv,
    c_send,
    c_recv,
    p_send,
    p_recv,
    zs_send,
    zs_recv,
):
    tile = lax.axis_index("tiles")
    freq = lax.axis_index("freq")
    parity = lax.rem(tile, 2)
    block = tile // 2
    partner = block * 2 + (1 - parity)
    per_dev = right_ref.shape[2]
    rows = right_ref.shape[3]
    half = rows // 2
    width = right_ref.shape[4]
    rank_width = width // 2
    cols = model_ref.shape[2]
    n_rows = n_tiles // 2

    def tile_at(k):
        return lax.rem(tile + k, n_tiles)

    def freq_at(k):
        return lax.rem(freq + k, n_freq)

    def row_far(k):
        upper = block // (n_rows // 2)
        first = (1 - upper) * (n_rows - 1 - k) + upper * k
        down = (block - first + n_rows) // n_rows
        up = (first - block + n_rows) // n_rows
        return first - (1 - upper) * down + upper * up

    freq_order = sorted(range(1, n_freq), key=lambda k: abs(k - n_freq // 2))

    own = pl.ds(pl.multiple_of(parity * half, half), half)
    other = pl.ds(pl.multiple_of((1 - parity) * half, half), half)
    own_slots = pl.ds(parity * per_dev, per_dev)
    inputs = [
        pltpu.make_async_copy(src, dst, in_sem.at[at])
        for at, (src, dst) in enumerate(
            [
                (right_hbm, right_ref),
                (rank_hbm, rank_ref),
                (model_hbm, model_ref),
                (map_hbm, map_ref),
                (left_hbm.at[0, 0, :, own, :], left_rows.at[own_slots]),
                (obs_hbm, obs_ref),
                (mix_hbm, mix_ref),
            ]
        )
    ]
    barrier = pltpu.get_barrier_semaphore()

    def greet(k):
        pl.semaphore_signal(
            barrier, inc=1, device_id=(tile_at(k + 1), freq), device_id_type=MESH
        )

    each(n_tiles - 1, greet)
    for k in range(1, n_freq):
        pl.semaphore_signal(barrier, inc=1, device_id=(tile, freq_at(k)), device_id_type=MESH)
    for one in inputs:
        one.start()
    inputs[0].wait()
    inputs[1].wait()
    lane = lax.rem(lax.broadcasted_iota(jnp.int32, (rows, width), 1), rank_width)

    def mask_right(s):
        keep = lane < rank_ref[0, 0, s]
        right_masked[s] = jnp.where(keep, right_ref[0, 0, s].astype(F32), 0.0).astype(BF16)

    each(per_dev, mask_right)
    pl.semaphore_wait(barrier, n_tiles - 1 + n_freq - 1)

    def copy(src, dst, send, recv, device):
        return pltpu.make_async_remote_copy(
            src_ref=src,
            dst_ref=dst,
            send_sem=send,
            recv_sem=recv,
            device_id=device,
            device_id_type=MESH,
        )

    x_copy = copy(model_hbm.at[0], x_other, pair_send.at[0], pair_recv.at[0], (partner, freq))
    x_copy.start()
    left_copy = copy(
        left_hbm.at[0, 0, :, other, :],
        left_rows.at[own_slots],
        pair_send.at[1],
        pair_recv.at[1],
        (partner, freq),
    )
    left_copy.start()

    def obs_copy(k, source):
        return copy(
            obs_hbm.at[0],
            obs_all.at[source],
            obs_send.at[k],
            obs_recv.at[source],
            (tile, freq_at(k)),
        )

    for k in range(1, n_freq):
        obs_copy(k, freq).start()

    inputs[2].wait()
    inputs[3].wait()
    x_copy.wait_recv()

    def right_coeffs(s):
        product = transposed_dot(right_masked[s, own, :], model_ref[0]) + transposed_dot(
            right_masked[s, other, :], x_other[...]
        )
        coeff_own[s] = conjugate_fold(product).astype(BF16)

    each(per_dev, right_coeffs)

    def place_coeffs(i):
        def term(s):
            hit = jnp.full((rank_width, cols), map_ref[0, s], jnp.int32) == i
            return jnp.where(hit, coeff_own[s].astype(F32), 0.0)

        coeff_send[i] = total(per_dev, term, jnp.zeros((rank_width, cols), F32)).astype(BF16)

    def c_copy(target, source):
        return copy(
            coeff_send.at[target // 2],
            coeff_got.at[source],
            c_send.at[target],
            c_recv.at[source],
            (target, freq),
        )

    def c_start(k):
        place_coeffs(row_far(k))
        c_copy(2 * row_far(k), tile).start()
        c_copy(2 * row_far(k) + 1, tile).start()

    each(n_rows - 1, c_start)
    place_coeffs(block)
    c_copy(partner, tile).start()
    coeff_got[tile] = coeff_send[block]

    def place_right(i):
        def term(rows_at):
            def one(s):
                hit = jnp.full((half, width), map_ref[0, s], jnp.int32) == i
                return jnp.where(hit, right_masked[s, rows_at, :].astype(F32), 0.0)

            return total(per_dev, one, jnp.zeros((half, width), F32)).astype(BF16)

        right_rows[0, i] = term(own)
        right_rows[1, i] = term(other)

    each(n_rows, place_right)
    right_copy = copy(
        right_rows.at[1], right_got, pair_send.at[2], pair_recv.at[2], (partner, freq)
    )

    for one in inputs[4:]:
        one.wait()
    left_copy.wait_recv()
    def forward_term(j):
        both = coeff_got[2 * j].astype(F32) + coeff_got[2 * j + 1].astype(F32)
        return jnp.dot(left_rows[j], stack_coeffs(both), preferred_element_type=F32)

    c_copy(partner, partner).wait_recv()
    pred = forward_term(block)

    def forward_near(k):
        j = row_far(n_rows - 2 - k)
        c_copy(2 * j, 2 * j).wait_recv()
        c_copy(2 * j + 1, 2 * j + 1).wait_recv()
        return forward_term(j)

    pred = total(n_rows - 1, forward_near, pred)
    pred_send[...] = pred.astype(BF16)

    def p_copy(k, source):
        return copy(
            pred_send,
            pred_got.at[source],
            p_send.at[k],
            p_recv.at[source],
            (tile, freq_at(k)),
        )

    for k in freq_order:
        p_copy(k, freq).start()
    right_copy.start()

    res = mix_ref[freq, freq] * pred - obs_ref[0].astype(F32)

    def gram(at):
        weight = mix_ref[0, freq] * mix_ref[0, at]
        for g in range(1, n_freq):
            weight = weight + mix_ref[g, freq] * mix_ref[g, at]
        return weight

    adjoint = gram(freq) * pred - mix_ref[freq, freq] * obs_ref[0].astype(F32)
    for k in range(1, n_freq):
        source = freq_at(k)
        obs_copy(k, source).wait_recv()
        adjoint = adjoint - mix_ref[source, freq] * obs_all[source].astype(F32)
    for k in range(1, n_freq):
        source = freq_at(k)
        p_copy(k, source).wait_recv()
        got = pred_got[source].astype(F32)
        res = res + mix_ref[freq, source] * got
        adjoint = adjoint + gram(source) * got
    adjoint_bf = adjoint.astype(BF16)

    def back(j):
        product = transposed_dot(left_rows[j], adjoint_bf)
        z_send[j] = conjugate_fold(product).astype(BF16)

    def z_copy(target, source):
        return copy(
            z_send.at[target // 2],
            z_got.at[source],
            zs_send.at[target],
            zs_recv.at[source],
            (target, freq),
        )

    def z_start(k):
        j = row_far(k)
        back(j)
        z_copy(2 * j, tile).start()
        z_copy(2 * j + 1, tile).start()

    each(n_rows - 1, z_start)
    back(block)
    z_copy(partner, tile).start()
    z_got[tile] = z_send[block]
    res_ref[0] = res

    right_copy.wait_recv()

    def merge_right(i):
        right_rows[0, i] = (right_rows[0, i].astype(F32) + right_got[i].astype(F32)).astype(BF16)

    each(n_rows, merge_right)
    def gradient_term(i):
        both = z_got[2 * i].astype(F32) + z_got[2 * i + 1].astype(F32)
        return jnp.dot(right_rows[0, i], stack_coeffs(both), preferred_element_type=F32)

    z_copy(partner, partner).wait_recv()
    grad = gradient_term(block)

    def gradient_near(k):
        i = row_far(n_rows - 2 - k)
        z_copy(2 * i, 2 * i).wait_recv()
        z_copy(2 * i + 1, 2 * i + 1).wait_recv()
        return gradient_term(i)

    grad_ref[0] = total(n_rows - 1, gradient_near, grad)

    x_copy.wait_send()
    left_copy.wait_send()
    right_copy.wait_send()
    for k in range(1, n_freq):
        obs_copy(k, freq).wait_send()
        p_copy(k, freq).wait_send()
    each(n_tiles - 1, lambda k: c_copy(tile_at(k + 1), tile).wait_send())
    each(n_tiles - 1, lambda k: z_copy(tile_at(k + 1), tile).wait_send())


def write_out(res_in, grad_in, res_out, grad_out, sem):
    copies = [
        pltpu.make_async_copy(res_in, res_out, sem.at[0]),
        pltpu.make_async_copy(grad_in, grad_out, sem.at[1]),
    ]
    for one in copies:
        one.start()
    for one in copies:
        one.wait()


def body(model_in, observed, right_factors, left_factors, tile_map, tile_ranks, window_mix):
    n_tiles = lax.axis_size("tiles")
    n_freq = lax.axis_size("freq")
    n_rows = n_tiles // 2
    per_dev, rows, width = right_factors.shape[2:]
    half = rows // 2
    cols = model_in.shape[2]
    rank = width // 2
    vmem = pl.BlockSpec(memory_space=pltpu.VMEM)
    hbm = pl.BlockSpec(memory_space=pl.ANY)
    dma = pltpu.SemaphoreType.DMA
    field = jax.ShapeDtypeStruct((1, half, cols), F32)
    results = pl.pallas_call(
        functools.partial(kernel, n_tiles, n_freq),
        out_shape=(field, field),
        in_specs=[hbm] * 7,
        out_specs=(vmem, vmem),
        scratch_shapes=[
            pltpu.SMEM(tile_map.shape, jnp.int32),
            pltpu.SMEM(tile_ranks.shape, jnp.int32),
            pltpu.SMEM(window_mix.shape, F32),
            pltpu.VMEM(model_in.shape, BF16),
            pltpu.VMEM(observed.shape, BF16),
            pltpu.VMEM(right_factors.shape, BF16),
            pltpu.VMEM((n_rows, half, width), BF16),
            dma((7,)),
            pltpu.VMEM((half, cols), BF16),
            pltpu.VMEM((n_freq, half, cols), BF16),
            pltpu.VMEM((per_dev, rows, width), BF16),
            pltpu.VMEM((2, n_rows, half, width), BF16),
            pltpu.VMEM((n_rows, half, width), BF16),
            pltpu.VMEM((per_dev, rank, cols), BF16),
            pltpu.VMEM((n_rows, rank, cols), BF16),
            pltpu.VMEM((n_tiles, rank, cols), BF16),
            pltpu.VMEM((half, cols), BF16),
            pltpu.VMEM((n_freq, half, cols), BF16),
            pltpu.VMEM((n_rows, rank, cols), BF16),
            pltpu.VMEM((n_tiles, rank, cols), BF16),
            dma((3,)),
            dma((3,)),
            dma((n_freq,)),
            dma((n_freq,)),
            dma((n_tiles,)),
            dma((n_tiles,)),
            dma((n_freq,)),
            dma((n_freq,)),
            dma((n_tiles,)),
            dma((n_tiles,)),
        ],
        compiler_params=pltpu.CompilerParams(
            collective_id=0, has_side_effects=True, vmem_limit_bytes=40 * 1024 * 1024
        ),
        name="deconvolve",
    )(*[pltpu.with_memory_space_constraint(a, pltpu.HBM) for a in (tile_map, tile_ranks, window_mix, model_in, observed, right_factors, left_factors)])
    return pl.pallas_call(
        write_out,
        out_shape=(field, field),
        in_specs=[vmem, vmem],
        out_specs=(hbm, hbm),
        scratch_shapes=[dma((2,))],
        name="write_out",
    )(*[pltpu.with_memory_space_constraint(a, pltpu.VMEM) for a in results])


def solution(mesh):
    placed = (
        P("freq", "tiles", None),
        P("freq", "tiles", None),
        P("freq", "tiles", None, None, None),
        P("freq", "tiles", None, None, None),
        P("tiles", None),
        P("freq", "tiles", None),
        P(),
    )
    return jax.shard_map(
        body,
        mesh=mesh,
        in_specs=placed,
        out_specs=(P("freq", "tiles", None), P("freq", "tiles", None)),
        check_vma=False,
    )
```
